512 devices in a mesh: dp: 16 (over y, core), expert: 32 (over x, z).
Axes of the slice: x: 4, y: 8, z: 8, core: 2. Of those that a mesh axis runs over, the one named last changes fastest.
Arguments:
- tokens: bfloat16 [2, 8192, 3584], P(None, ('dp', 'expert')), parts along dimension 1, may hold values from -6 to 6
- expert_ids: int32 [2, 8192, 2], P(None, ('dp', 'expert')), parts along dimension 1, may hold values from 0 to 3, as said below
- route_weights: float32 [2, 8192, 2], P(None, ('dp', 'expert')), parts along dimension 1, may hold values from 0.4 to 2
- owner_map: int32 [64], P('dp'), parts along dimension 0, may hold values from 0 to 3, each once
- expert_weights: bfloat16 [4096, 3, 3584], P('expert'), may hold values from -0.09375 to 0.09375
Outputs:
- mixed: bfloat16 [2, 8192, 3584], P(None, ('dp', 'expert')), parts along dimension 1
The draws below stay inside these ranges and needn't reach their ends.
There are 16 independent parts, one for each index of `dp`. The reference program is written for one: setup_inputs(seed, part) draws one part's arguments, and reference() takes and returns one part's arrays. A program takes and returns all parts, laid end to end along the dimension named above; an argument that names none is the same for every part. Nothing has to cross between parts.
Inputs may be any that keep to these rules, and one draw needn't show every extreme that they name: `expert_ids`: each token names 2 different experts. One expert, the same for all steps and devices of a part, is named by at least 8 of the tokens of every device in every step, by all 16 tokens of some device in some step, and by more of the tokens of every device over the 2 steps together than any other expert; every other expert is named by at most 8 tokens of one device in one step, a bound reached in every draw. `owner_map`: each group owns exactly one expert.
All inputs are finite; a program needn't handle non-finite values.
Results may differ from the reference program's by a relative error of at most 0.006.
Values may be sent and summed in bfloat16 or wider, within the bound.
No kernel may reach another device: no remote copies, remote signals or barrier semaphores. Data moves between devices by JAX's collectives and lax.ppermute only.
A program may use at most 64 MiB of HBM per device.

```python
import jax
import jax.numpy as jnp
from jax import lax

D = 3584
HIDDEN_SIZE = 1024
EXPERTS = 4
TOP = 2
STEPS = 2
ROWS = 16
TOKENS = 512
N_EXPERT = 32


def draw_expert_ids(key, part):
    block_count = STEPS * (TOKENS // ROWS)
    subkeys = jax.random.split(jax.random.fold_in(key, 23), 6)
    hot_expert = jax.random.randint(subkeys[0], (), 0, EXPERTS)
    lacking = jax.random.randint(subkeys[1], (block_count,), 0, ROWS // 2)
    first_block = jax.random.randint(subkeys[2], (), 0, block_count)
    block_index = jnp.arange(block_count)
    lacking = jnp.where(block_index == first_block, ROWS // 2, lacking)
    lacking = jnp.where(block_index == (first_block + 1) % block_count, 0, lacking)
    orders = jax.vmap(lambda subkey: jax.random.permutation(subkey, ROWS))(jax.random.split(subkeys[3], block_count))
    lacks_hot = orders < lacking[:, None]
    consumed = jnp.where(lacks_hot, 2, 1)
    start_slot = jnp.cumsum(consumed, axis=1) - consumed
    offsets = jax.random.randint(subkeys[4], (block_count, 1), 0, EXPERTS - 1)
    first_cold = (hot_expert + 1 + (offsets + start_slot) % (EXPERTS - 1)) % EXPERTS
    second_cold = (hot_expert + 1 + (offsets + start_slot + 1) % (EXPERTS - 1)) % EXPERTS
    pick_first = jnp.where(lacks_hot, first_cold, hot_expert)
    pick_second = jnp.where(lacks_hot, second_cold, first_cold)
    flipped = jax.random.randint(subkeys[5], (block_count, ROWS), 0, 2) == 1
    leading = jnp.where(flipped, pick_second, pick_first)
    trailing = jnp.where(flipped, pick_first, pick_second)
    return jnp.stack([leading, trailing], axis=-1).reshape(STEPS, TOKENS, TOP).astype(jnp.int32)


def block_levels(rng, dims, shards, least, high):
    def one(axis_at, parts):
        draws = jax.random.uniform(jax.random.fold_in(jax.random.fold_in(rng, 6), axis_at), (parts,), jnp.float32, least / len(shards), high / len(shards))
        return jnp.repeat(jnp.exp(draws), dims[axis_at] // parts).reshape((-1,) + (1,) * (len(dims) - axis_at - 1))

    factor_of = one(*shards[0])
    for cut in shards[1:]:
        factor_of = factor_of * one(*cut)
    return factor_of


def bell_draw(key, extent, width, most, shards=(), dtype=jnp.bfloat16):
    factor_of = block_levels(key, extent, shards, -0.22, 0.18) if shards else 1.0
    result = jax.random.normal(key, extent, jnp.float32) * width * factor_of
    return jnp.minimum(jnp.maximum(result, -most), most).astype(dtype)


def setup_inputs(seed: int = 0, part: int = 0) -> dict:
    key_of = jax.random.split(jax.random.key(seed), 6)
    own_keys = jax.random.split(jax.random.fold_in(key_of[5], part), 6)
    tokens = bell_draw(own_keys[0], (STEPS, TOKENS, D), 1.0, 6.0, ((1, 32),))
    expert_ids = draw_expert_ids(jax.random.fold_in(jax.random.fold_in(key_of[5], part), 71), part)
    route_weights = jnp.clip(0.4 + 1.6 * jax.random.uniform(own_keys[2], (STEPS, TOKENS, TOP), jnp.float32) ** block_levels(own_keys[2], (STEPS, TOKENS, TOP), ((1, 32),), -0.2, 0.2), 0.4, 2.0)
    owner_map = jax.random.permutation(own_keys[3], EXPERTS).astype(jnp.int32)
    expert_weights = bell_draw(key_of[4], (EXPERTS * HIDDEN_SIZE, 3, D), D ** -0.5, 0.09375, ((0, 32),))
    return {"tokens": tokens, "expert_ids": expert_ids, "route_weights": route_weights, "owner_map": owner_map, "expert_weights": expert_weights}


def reference(tokens, expert_ids, route_weights, owner_map, expert_weights):
    copies = N_EXPERT // EXPERTS
    slice_width = HIDDEN_SIZE // copies
    flat_tokens = tokens.reshape(-1, D)
    flat_ids = expert_ids.reshape(-1, TOP)
    flat_route = route_weights.reshape(-1, TOP)
    running_sum = jnp.zeros((flat_tokens.shape[0], D), jnp.float32)
    for group_index in range(EXPERTS):
        owned_expert = jnp.sum(jnp.where(owner_map == group_index, jnp.arange(EXPERTS).astype(jnp.int32), 0)).astype(jnp.int32)
        group_weights = expert_weights[group_index * HIDDEN_SIZE:(group_index + 1) * HIDDEN_SIZE]
        gate = jnp.dot(flat_tokens, group_weights[:, 0, :].T, preferred_element_type=jnp.float32)
        upward = jnp.dot(flat_tokens, group_weights[:, 1, :].T, preferred_element_type=jnp.float32)
        hidden = (jax.nn.silu(gate) * upward).astype(jnp.bfloat16)
        slice_parts = jnp.einsum("nkh,khd->nkd", hidden.reshape(-1, copies, slice_width).astype(jnp.float32),
                                 group_weights[:, 2, :].reshape(copies, slice_width, D).astype(jnp.float32),
                                 precision=lax.Precision.HIGHEST)
        rounded = lax.optimization_barrier(slice_parts.astype(jnp.bfloat16))
        expert_out = jnp.sum(rounded.astype(jnp.float32), axis=1)
        coefficient = jnp.sum(jnp.where(flat_ids == owned_expert, flat_route, 0.0), axis=1)
        running_sum = running_sum + coefficient[:, None] * expert_out
    return running_sum.astype(jnp.bfloat16).reshape(tokens.shape)
```

```python
import jax
import jax.numpy as jnp
from jax import lax
from jax.sharding import Mesh, PartitionSpec as P

EXPERTS = 4
AXES = ("y", "core", "x", "z")


def from_offset(block, axis, offset):
    size = lax.axis_size(axis)
    return lax.ppermute(block, axis, [((i + offset) % size, i) for i in range(size)])


def narrow(values):
    return lax.reduce_precision(values, 8, 7)


def packed_tokens(tokens, expert_ids, route_weights, owner_map):
    rows = tokens.shape[0] * tokens.shape[1]
    groups = jnp.arange(EXPERTS)
    group = jnp.sum(jnp.where(expert_ids[..., None] == groups, owner_map, 0), axis=-1)
    coef = jnp.sum(
        jnp.where(group[..., None] == groups, route_weights[..., None], 0.0), axis=2
    ).reshape(rows, EXPERTS)
    high = narrow(coef)
    middle = narrow(coef - high)
    low = coef - high - middle
    tail = jnp.concatenate([high, middle, low, jnp.zeros((rows, 116), jnp.float32)], axis=1)
    return jnp.concatenate([tokens.reshape(rows, -1), tail.astype(jnp.bfloat16)], axis=1)


def gathered_tokens(own):
    up2 = from_offset(own, "z", 2)
    down2 = from_offset(own, "z", -2)
    far = from_offset(own, "z", 4)
    up13 = from_offset(jnp.concatenate([own, up2]), "z", 1)
    down13 = from_offset(jnp.concatenate([own, down2]), "z", -1)
    return jnp.concatenate([own, up13, down13, up2, down2, far])


def other_experts(planes, core, parity):
    count, width = len(planes), planes[0].shape[1]
    start = core * 64 + parity * 32
    mine = [lax.dynamic_slice_in_dim(plane, start, 32, 0) for plane in planes]
    sent = jnp.stack(mine)
    three = jnp.stack([from_offset(sent, "x", k) for k in (1, -1, 2)], axis=1)
    three = three.reshape(count, 96, width)
    if count == 2:
        a = from_offset(three[0], "y", -1)
        b = from_offset(three[1], "y", 1)
        half = jnp.stack([three, jnp.stack([a, b])], axis=1)
    else:
        a = from_offset(three[0, :48], "y", -1)
        b = from_offset(three[0, 48:], "y", 1)
        half = jnp.stack([three, jnp.concatenate([a, b])[None]], axis=1)
    half = half.reshape(count, 192, width)
    other = from_offset(half, "core", 1)
    return [jnp.concatenate([planes[k], half[k], other[k]]) for k in range(count)]


def returned(part):
    rows = part.shape[0] // 8
    own, up13, down13, up2, down2, far = (
        part[:rows], part[rows:3 * rows], part[3 * rows:5 * rows],
        part[5 * rows:6 * rows], part[6 * rows:7 * rows], part[7 * rows:])
    from_down = from_offset(up13, "z", -1)
    from_up = from_offset(down13, "z", 1)
    from_far = from_offset(far, "z", 4)
    wide = lambda v: v.astype(jnp.float32)
    sum_up2 = (wide(up2) + wide(from_down[rows:])).astype(jnp.bfloat16)
    sum_down2 = (wide(down2) + wide(from_up[rows:])).astype(jnp.bfloat16)
    from_down2 = from_offset(sum_up2, "z", -2)
    from_up2 = from_offset(sum_down2, "z", 2)
    return (wide(own) + wide(from_down[:rows]) + wide(from_up[:rows]) + wide(from_far)
            + wide(from_down2) + wide(from_up2)).astype(jnp.bfloat16)


def selector(x_index, hidden):
    position = jnp.arange(hidden)
    offset = jnp.where(position < 128, 0, 0)
    third = (position - 128) // 32 % 3
    offset = jnp.where(position < 128, 0, jnp.where(third == 0, 1, jnp.where(third == 1, 3, 2)))
    group = (x_index + offset) % EXPERTS
    row = jnp.arange(128)[:, None]
    return ((row < 12) & (row % EXPERTS == group[None, :])).astype(jnp.bfloat16)


def dot_t(a, b):
    return lax.dot_general(a, b, (((1,), (1,)), ((), ())), preferred_element_type=jnp.float32)


def shards(tokens, expert_ids, route_weights, owner_map, expert_weights):
    width = tokens.shape[-1]
    core, x_index, parity = lax.axis_index("core"), lax.axis_index("x"), lax.axis_index("y") % 2
    planes = [expert_weights[:, k, :] for k in range(3)]
    packed = packed_tokens(tokens, expert_ids, route_weights, owner_map)
    gate_rows, up_rows = other_experts(planes[:2], core, parity)
    (down_rows,) = other_experts(planes[2:], core, parity)
    gathered = gathered_tokens(packed)
    token_rows = gathered[:, :width]
    coef = jnp.dot(gathered[:, width:], selector(x_index, gate_rows.shape[0]),
                   preferred_element_type=jnp.float32)
    gate = dot_t(token_rows, gate_rows)
    up = dot_t(token_rows, up_rows)
    hidden = (narrow(jax.nn.silu(gate) * up) * coef).astype(jnp.bfloat16)
    part = jnp.dot(hidden, down_rows, preferred_element_type=jnp.float32).astype(jnp.bfloat16)
    return returned(part).reshape(tokens.shape)


def solution(mesh):
    split = Mesh(mesh.devices.reshape(8, 2, 4, 8), AXES)
    rows = P(None, AXES, None)
    return jax.shard_map(
        shards,
        mesh=split,
        in_specs=(rows, rows, rows, P(AXES[:2]), P(AXES[2:], None, None)),
        out_specs=rows,
        check_vma=False,
    )
```

```python
import jax
import jax.numpy as jnp
from jax import lax
from jax.experimental import pallas as pl
from jax.experimental.pallas import tpu as pltpu
from jax.sharding import Mesh, PartitionSpec as P


EXPERTS = 4
ROWS = 32
CHUNK = 512
AXES = ("y", "core", "x", "z")
OFFSETS = (0, 1, 3, -1, -3, 2, -2, 4)


def from_offset(block, axis, offset):
    size = lax.axis_size(axis)
    return lax.ppermute(block, axis, [((i + offset) % size, i) for i in range(size)])


def narrow(values):
    return lax.reduce_precision(values, 8, 7)


def packed_tokens(tokens, expert_ids, route_weights, owner_map):
    rows = tokens.shape[0] * tokens.shape[1]
    groups = jnp.arange(EXPERTS)
    group = jnp.sum(jnp.where(expert_ids[..., None] == groups, owner_map, 0), axis=-1)
    coef = jnp.sum(
        jnp.where(group[..., None] == groups, route_weights[..., None], 0.0), axis=2
    ).reshape(rows, EXPERTS)
    high = narrow(coef)
    middle = narrow(coef - high)
    low = coef - high - middle
    tail = jnp.concatenate([high, middle, low, jnp.zeros((rows, 116), jnp.float32)], axis=1)
    return jnp.concatenate([tokens.reshape(rows, -1), tail.astype(jnp.bfloat16)], axis=1)


def gathered_tokens(own):
    rows, width = own.shape
    sent = jnp.broadcast_to(own[None], (8, rows, width))
    return lax.all_to_all(sent, "z", split_axis=0, concat_axis=0, tiled=True)


def gate_up_pieces(weights, start):
    width = weights.shape[2]
    sent = lax.dynamic_slice(weights, (start, 0, 0), (32, 2, width)).transpose(1, 0, 2)
    arrived = [from_offset(sent, "x", k) for k in (1, 3, 2)]
    gate = jnp.concatenate([a[0] for a in arrived])
    up = jnp.concatenate([a[1] for a in arrived])
    more_gate = from_offset(gate, "y", -1)
    more_up = from_offset(up, "y", 1)
    half = jnp.concatenate([gate, more_gate, up, more_up])
    return half, from_offset(half, "core", 1)


def down_pieces(weights, start):
    width = weights.shape[2]
    sent = lax.dynamic_slice(weights, (start, 2, 0), (32, 1, width)).reshape(32, width)
    first, second, third = [from_offset(sent, "x", k) for k in (1, 3, 2)]
    lower = jnp.concatenate([first, second[:16]])
    upper = jnp.concatenate([second[16:], third])
    more_lower = from_offset(lower, "y", -1)
    more_upper = from_offset(upper, "y", 1)
    half = jnp.concatenate([lower, upper, more_lower, more_upper])
    return half, from_offset(half, "core", 1)


def dot_t(a, b):
    return lax.dot_general(a, b, (((1,), (1,)), ((), ())), preferred_element_type=jnp.float32)


def hidden_body(place, token_ref, tail_ref, own_ref, half_ref, other_ref, hidden_ref, gate_acc, up_acc):
    step = pl.program_id(0)
    x_index, z_index = place[0], place[1]
    sources = [lax.rem(z_index + (k + 8), 8) for k in OFFSETS]
    rows = jnp.concatenate([token_ref[s] for s in sources])
    gate_rows = jnp.concatenate([own_ref[0], half_ref[0], other_ref[0]])
    up_rows = jnp.concatenate([own_ref[1], half_ref[1], other_ref[1]])
    gate = dot_t(rows, gate_rows)
    up = dot_t(rows, up_rows)

    @pl.when(step == 0)
    def _():
        gate_acc[...] = gate
        up_acc[...] = up

    @pl.when(step > 0)
    def _():
        gate_acc[...] += gate
        up_acc[...] += up

    @pl.when(step == pl.num_programs(0) - 1)
    def _():
        tail = jnp.concatenate([tail_ref[s] for s in sources])
        position = lax.broadcasted_iota(jnp.int32, (128, 512), 1)
        row = lax.broadcasted_iota(jnp.int32, (128, 512), 0)
        third = lax.rem(lax.div(position, 32), 3)
        offset = jnp.where(position < 128, 0, jnp.where(third == 1, 1, jnp.where(third == 2, 3, 2)))
        group = lax.rem(x_index + offset, EXPERTS)
        chosen = (row < 3 * EXPERTS) & (lax.rem(row, EXPERTS) == group)
        coef = jnp.dot(tail, chosen.astype(jnp.bfloat16), preferred_element_type=jnp.float32)
        gate_all = gate_acc[...]
        hidden = gate_all / (1.0 + jnp.exp(-gate_all)) * up_acc[...]
        hidden = hidden.astype(jnp.bfloat16).astype(jnp.float32)
        hidden_ref[...] = (hidden * coef).astype(jnp.bfloat16)


def hidden_units(place, gathered, planes, half, other):
    width = planes.shape[2]
    steps = width // CHUNK
    spec = lambda shape: pl.BlockSpec(shape, lambda i, place: (0, 0, i))
    half, other = half.reshape(2, 192, width), other.reshape(2, 192, width)
    return pl.pallas_call(
        hidden_body,
        out_shape=jax.ShapeDtypeStruct((8 * ROWS, 512), jnp.bfloat16),
        grid_spec=pltpu.PrefetchScalarGridSpec(
            num_scalar_prefetch=1,
            grid=(steps,),
            in_specs=[
                spec((8, ROWS, CHUNK)),
                pl.BlockSpec((8, ROWS, 128), lambda i, place: (0, 0, width // 128)),
                spec((2, 128, CHUNK)),
                spec((2, 192, CHUNK)),
                spec((2, 192, CHUNK)),
            ],
            out_specs=pl.BlockSpec((8 * ROWS, 512), lambda i, place: (0, 0)),
            scratch_shapes=[pltpu.VMEM((8 * ROWS, 512), jnp.float32)] * 2,
        ),
        cost_estimate=pl.CostEstimate(
            flops=2 * 256 * 1024 * 3584, bytes_accessed=9_500_000, transcendentals=256 * 512
        ),
    )(place, gathered, gathered, planes, half, other)


def down_body(hidden_ref, own_ref, half_ref, other_ref, keep, up13, down13, up2, down2, far):
    rows = jnp.concatenate([own_ref[0], half_ref[...], other_ref[...]])
    part = jnp.dot(hidden_ref[...], rows, preferred_element_type=jnp.float32).astype(jnp.bfloat16)
    at = 0
    for ref in (keep, up13, down13, up2, down2, far):
        count = ref.shape[0]
        ref[...] = part[at:at + count]
        at += count


def down_parts(hidden, planes, half, other):
    width = planes.shape[2]
    spec = lambda rows: pl.BlockSpec((rows, CHUNK), lambda i: (0, i))
    counts = (ROWS, 2 * ROWS, 2 * ROWS, ROWS, ROWS, ROWS)
    return pl.pallas_call(
        down_body,
        out_shape=[jax.ShapeDtypeStruct((count, width), jnp.bfloat16) for count in counts],
        grid=(width // CHUNK,),
        in_specs=[
            pl.BlockSpec((8 * ROWS, 512), lambda i: (0, 0)),
            pl.BlockSpec((1, 128, CHUNK), lambda i: (2, 0, i)),
            spec(192),
            spec(192),
        ],
        out_specs=[spec(count) for count in counts],
        cost_estimate=pl.CostEstimate(
            flops=2 * 256 * 512 * 3584, bytes_accessed=5_500_000, transcendentals=0
        ),
    )(hidden, planes, half, other)


def returned(keep, up13, down13, up2, down2, far):
    rows = keep.shape[0]
    even = lax.axis_index("z") % 2 == 0
    wide = lambda v: v.astype(jnp.float32)
    pairs = [(i, (i + 2) % 8 if i % 2 == 0 else (i - 2) % 8) for i in range(8)]
    far = wide(lax.ppermute(far, "z", pairs))
    from_up = from_offset(down13, "z", 1)
    from_down = from_offset(up13, "z", -1)
    sum_up2 = wide(up2) + wide(from_down[rows:]) + jnp.where(even, far, 0.0)
    sum_down2 = wide(down2) + wide(from_up[rows:]) + jnp.where(even, 0.0, far)
    from_up2 = from_offset(sum_down2.astype(jnp.bfloat16), "z", 2)
    from_down2 = from_offset(sum_up2.astype(jnp.bfloat16), "z", -2)
    return (wide(keep) + wide(from_down[:rows]) + wide(from_up[:rows])
            + wide(from_down2) + wide(from_up2)).astype(jnp.bfloat16)


def shards(tokens, expert_ids, route_weights, owner_map, expert_weights):
    core, parity = lax.axis_index("core"), lax.axis_index("y") % 2
    start = core * 64 + parity * 32
    place = jnp.stack([lax.axis_index("x"), lax.axis_index("z")]).astype(jnp.int32)
    packed = packed_tokens(tokens, expert_ids, route_weights, owner_map)
    planes = expert_weights.transpose(1, 0, 2)
    half, other = gate_up_pieces(expert_weights, start)
    down_half, down_other = down_pieces(expert_weights, start)
    gathered = gathered_tokens(packed)
    hidden = hidden_units(place, gathered, planes, half, other)
    parts = down_parts(hidden, planes, down_half, down_other)
    return returned(*parts).reshape(tokens.shape)


def solution(mesh):
    split = Mesh(mesh.devices.reshape(8, 2, 4, 8), AXES)
    rows = P(None, AXES, None)
    return jax.shard_map(
        shards,
        mesh=split,
        in_specs=(rows, rows, rows, P(AXES[:2]), P(AXES[2:], None, None)),
        out_specs=rows,
        check_vma=False,
    )
```

```python
import jax
import jax.numpy as jnp
from jax import lax
from jax.sharding import Mesh, PartitionSpec as P


EXPERTS = 4
ROWS = 32
AXES = ("y", "core", "x", "z")


def from_offset(block, axis, offset):
    size = lax.axis_size(axis)
    return lax.ppermute(block, axis, [((i + offset) % size, i) for i in range(size)])


def narrow(values):
    return lax.reduce_precision(values, 8, 7)


def packed_tokens(tokens, expert_ids, route_weights, owner_map):
    rows = tokens.shape[0] * tokens.shape[1]
    groups = jnp.arange(EXPERTS)
    group = jnp.sum(jnp.where(expert_ids[..., None] == groups, owner_map, 0), axis=-1)
    coef = jnp.sum(
        jnp.where(group[..., None] == groups, route_weights[..., None], 0.0), axis=2
    ).reshape(rows, EXPERTS)
    high = narrow(coef)
    middle = narrow(coef - high)
    low = coef - high - middle
    tail = jnp.concatenate([high, middle, low, jnp.zeros((rows, 116), jnp.float32)], axis=1)
    return jnp.concatenate([tokens.reshape(rows, -1), tail.astype(jnp.bfloat16)], axis=1)


def gathered_tokens(own):
    up2 = from_offset(own, "z", 2)
    down2 = from_offset(own, "z", -2)
    far = from_offset(own, "z", 4)
    up13 = from_offset(jnp.concatenate([own, up2]), "z", 1)
    down13 = from_offset(jnp.concatenate([own, down2]), "z", -1)
    return jnp.concatenate([own, up13, down13, up2, down2, far])


def gate_up_pieces(weights, start):
    width = weights.shape[2]
    sent = lax.dynamic_slice(weights, (start, 0, 0), (32, 2, width)).transpose(1, 0, 2)
    arrived = [from_offset(sent, "x", k) for k in (1, 3, 2)]
    three = jnp.stack(arrived, axis=1).reshape(2, 96, width)
    gate, up = three[0], three[1]
    more = [from_offset(gate, "y", -1), from_offset(up, "y", 1)]
    half = jnp.stack([three, jnp.stack(more)], axis=1).reshape(384, width)
    return half, from_offset(half, "core", 1)


def down_pieces(weights, start, rest):
    width = weights.shape[2]
    sent = jnp.stack(
        [lax.dynamic_slice(weights, (row, 2, 0), (32, 1, width)).reshape(32, width) for row in (start, rest)]
    )
    arrived = [from_offset(sent, "x", k) for k in (1, 3, 2)]
    half = jnp.stack(arrived, axis=1).reshape(192, width)
    return half, from_offset(half, "core", 1)


def dot_t(a, b):
    return lax.dot_general(a, b, (((1,), (1,)), ((), ())), preferred_element_type=jnp.float32)


def coefficients(x_index, tail):
    position = jnp.arange(512)
    third = position // 32 % 3
    offset = jnp.where(position < 128, 0, jnp.where(third == 1, 1, jnp.where(third == 2, 3, 2)))
    group = (x_index + offset) % EXPERTS
    column = jnp.arange(128)
    chosen = (column < 3 * EXPERTS) & (column % EXPERTS == group[:, None])
    return dot_t(chosen.astype(jnp.bfloat16), tail)


def hidden_units(coef, tokens, own, half, other):
    first, second, third = dot_t(own, tokens), dot_t(half, tokens), dot_t(other, tokens)
    gate = jnp.concatenate([first[:128], second[:192], third[:192]])
    up = jnp.concatenate([first[128:], second[192:], third[192:]])
    hidden = narrow(gate / (1.0 + jnp.exp(-gate)) * up)
    return (hidden * coef).astype(jnp.bfloat16)


def returned(hidden, own, half, other):
    rows = jnp.concatenate([own, half, other])
    part = lax.dot_general(hidden, rows, (((0,), (0,)), ((), ())), preferred_element_type=jnp.float32)
    keep, up1, up3, down1, down3, up2, down2, far = part.astype(jnp.bfloat16).reshape(8, ROWS, -1)
    even = lax.axis_index("z") % 2 == 0
    wide = lambda v: v.astype(jnp.float32)
    pairs = [(i, (i + 2) % 8 if i % 2 == 0 else (i - 2) % 8) for i in range(8)]
    far = wide(lax.ppermute(far, "z", pairs))
    from_up3 = from_offset(down3, "z", 1)
    from_down3 = from_offset(up3, "z", -1)
    from_up1 = from_offset(down1, "z", 1)
    from_down1 = from_offset(up1, "z", -1)
    sum_up2 = wide(up2) + wide(from_down3) + jnp.where(even, far, 0.0)
    sum_down2 = wide(down2) + wide(from_up3) + jnp.where(even, 0.0, far)
    from_up2 = from_offset(sum_down2.astype(jnp.bfloat16), "z", 2)
    from_down2 = from_offset(sum_up2.astype(jnp.bfloat16), "z", -2)
    return (wide(keep) + wide(from_down1) + wide(from_up1)
            + wide(from_down2) + wide(from_up2)).astype(jnp.bfloat16)


def shards(tokens, expert_ids, route_weights, owner_map, expert_weights):
    width = tokens.shape[-1]
    core, parity, x_index = lax.axis_index("core"), lax.axis_index("y") % 2, lax.axis_index("x")
    start, rest = core * 64 + parity * 32, core * 64 + 32 - parity * 32
    packed = packed_tokens(tokens, expert_ids, route_weights, owner_map)
    planes = expert_weights.transpose(1, 0, 2)
    half, other = gate_up_pieces(expert_weights, start)
    down_half, down_other = down_pieces(expert_weights, start, rest)
    gathered = gathered_tokens(packed)
    coef = coefficients(x_index, gathered[:, width:])
    own = planes[:2].reshape(256, width)
    hidden = hidden_units(coef, gathered[:, :width], own, half, other)
    return returned(hidden, planes[2], down_half, down_other).reshape(tokens.shape)


def solution(mesh):
    split = Mesh(mesh.devices.reshape(8, 2, 4, 8), AXES)
    rows = P(None, AXES, None)
    return jax.shard_map(
        shards,
        mesh=split,
        in_specs=(rows, rows, rows, P(AXES[:2]), P(AXES[2:], None, None)),
        out_specs=rows,
        check_vma=False,
    )
```

```python
import jax
import jax.numpy as jnp
from jax import lax
from jax.sharding import Mesh, PartitionSpec as P


EXPERTS = 4
ROWS = 32
AXES = ("y", "core", "x", "z")


def from_offset(block, axis, offset):
    size = lax.axis_size(axis)
    return lax.ppermute(block, axis, [((i + offset) % size, i) for i in range(size)])


def narrow(values):
    return lax.reduce_precision(values, 8, 7)


def packed_tokens(tokens, expert_ids, route_weights, owner_map):
    rows = tokens.shape[0] * tokens.shape[1]
    groups = jnp.arange(EXPERTS)
    group = jnp.sum(jnp.where(expert_ids[..., None] == groups, owner_map, 0), axis=-1)
    coef = jnp.sum(
        jnp.where(group[..., None] == groups, route_weights[..., None], 0.0), axis=2
    ).reshape(rows, EXPERTS)
    high = narrow(coef)
    middle = narrow(coef - high)
    low = coef - high - middle
    tail = jnp.concatenate([high, middle, low, jnp.zeros((rows, 116), jnp.float32)], axis=1)
    return jnp.concatenate([tokens.reshape(rows, -1), tail.astype(jnp.bfloat16)], axis=1)


def gathered_tokens(own):
    up2 = from_offset(own, "z", 2)
    down2 = from_offset(own, "z", -2)
    far = from_offset(own, "z", 4)
    up13 = from_offset(jnp.concatenate([own, up2]), "z", 1)
    down13 = from_offset(jnp.concatenate([own, down2]), "z", -1)
    return jnp.concatenate([own, up13, down13, up2, down2, far])


def gate_up_pieces(weights, start):
    width = weights.shape[2]
    sent = lax.dynamic_slice(weights, (start, 0, 0), (32, 2, width)).transpose(1, 0, 2)
    arrived = [from_offset(sent, "x", k) for k in (1, 3, 2)]
    three = jnp.stack(arrived, axis=1).reshape(2, 96, width)
    gate, up = three[0], three[1]
    more = [from_offset(gate, "y", -1), from_offset(up, "y", 1)]
    half = jnp.stack([three, jnp.stack(more)], axis=1).reshape(384, width)
    return half, from_offset(half, "core", 1)


def down_pieces(weights, start, rest):
    width = weights.shape[2]
    sent = jnp.stack(
        [lax.dynamic_slice(weights, (row, 2, 0), (32, 1, width)).reshape(32, width) for row in (start, rest)]
    )
    arrived = [from_offset(sent, "x", k) for k in (1, 3, 2)]
    half = jnp.stack(arrived, axis=1).reshape(192, width)
    return half, from_offset(half, "core", 1)


def dot_t(a, b):
    return lax.dot_general(a, b, (((1,), (1,)), ((), ())), preferred_element_type=jnp.float32)


def coefficients(x_index, tail):
    position = jnp.arange(512)
    third = position // 32 % 3
    offset = jnp.where(position < 128, 0, jnp.where(third == 1, 1, jnp.where(third == 2, 3, 2)))
    group = (x_index + offset) % EXPERTS
    column = jnp.arange(128)
    chosen = (column < 3 * EXPERTS) & (column % EXPERTS == group[:, None])
    return dot_t(chosen.astype(jnp.bfloat16), tail)


def gated(product, coef):
    rows = product.shape[0] // 2
    gate, up = product[:rows], product[rows:]
    return (narrow(gate / (1.0 + jnp.exp(-gate)) * up) * coef).astype(jnp.bfloat16)


def hidden_units(coef, tokens, own, half, other):
    first = dot_t(own, tokens)
    second, third = dot_t(half, tokens), dot_t(other, tokens)
    return jnp.concatenate(
        [gated(first, coef[:128]), gated(second, coef[128:320]), gated(third, coef[320:])]
    )


def returned(hidden, own, half, other):
    rows = jnp.concatenate([own, half, other])
    part = lax.dot_general(hidden, rows, (((0,), (0,)), ((), ())), preferred_element_type=jnp.float32)
    keep, up1, up3, down1, down3, up2, down2, far = part.astype(jnp.bfloat16).reshape(8, ROWS, -1)
    even = lax.axis_index("z") % 2 == 0
    wide = lambda v: v.astype(jnp.float32)
    pairs = [(i, (i + 2) % 8 if i % 2 == 0 else (i - 2) % 8) for i in range(8)]
    far = wide(lax.ppermute(far, "z", pairs))
    from_up3 = from_offset(down3, "z", 1)
    from_down3 = from_offset(up3, "z", -1)
    from_up1 = from_offset(down1, "z", 1)
    from_down1 = from_offset(up1, "z", -1)
    sum_up2 = wide(up2) + wide(from_down3) + jnp.where(even, far, 0.0)
    sum_down2 = wide(down2) + wide(from_up3) + jnp.where(even, 0.0, far)
    from_up2 = from_offset(sum_down2.astype(jnp.bfloat16), "z", 2)
    from_down2 = from_offset(sum_up2.astype(jnp.bfloat16), "z", -2)
    return (wide(keep) + wide(from_down1) + wide(from_up1)
            + wide(from_down2) + wide(from_up2)).astype(jnp.bfloat16)


def shards(tokens, expert_ids, route_weights, owner_map, expert_weights):
    width = tokens.shape[-1]
    core, parity, x_index = lax.axis_index("core"), lax.axis_index("y") % 2, lax.axis_index("x")
    start, rest = core * 64 + parity * 32, core * 64 + 32 - parity * 32
    packed = packed_tokens(tokens, expert_ids, route_weights, owner_map)
    planes = expert_weights.transpose(1, 0, 2)
    half, other = gate_up_pieces(expert_weights, start)
    down_half, down_other = down_pieces(expert_weights, start, rest)
    gathered = gathered_tokens(packed)
    coef = coefficients(x_index, gathered[:, width:])
    own = planes[:2].reshape(256, width)
    hidden = hidden_units(coef, gathered[:, :width], own, half, other)
    return returned(hidden, planes[2], down_half, down_other).reshape(tokens.shape)


def solution(mesh):
    split = Mesh(mesh.devices.reshape(8, 2, 4, 8), AXES)
    rows = P(None, AXES, None)
    return jax.shard_map(
        shards,
        mesh=split,
        in_specs=(rows, rows, rows, P(AXES[:2]), P(AXES[2:], None, None)),
        out_specs=rows,
        check_vma=False,
    )
```

```python
import jax
import jax.numpy as jnp
from jax import lax
from jax.sharding import Mesh, PartitionSpec as P


EXPERTS = 4
ROWS = 32
AXES = ("y", "core", "x", "z")


def from_offset(block, axis, offset):
    size = lax.axis_size(axis)
    return lax.ppermute(block, axis, [((i + offset) % size, i) for i in range(size)])


def narrow(values):
    return lax.reduce_precision(values, 8, 7)


def packed_tokens(tokens, expert_ids, route_weights, owner_map):
    rows = tokens.shape[0] * tokens.shape[1]
    groups = jnp.arange(EXPERTS)
    group = jnp.sum(jnp.where(expert_ids[..., None] == groups, owner_map, 0), axis=-1)
    coef = jnp.sum(
        jnp.where(group[..., None] == groups, route_weights[..., None], 0.0), axis=2
    ).reshape(rows, EXPERTS)
    high = narrow(coef)
    middle = narrow(coef - high)
    low = coef - high - middle
    tail = jnp.concatenate([high, middle, low, jnp.zeros((rows, 116), jnp.float32)], axis=1)
    return jnp.concatenate([tokens.reshape(rows, -1), tail.astype(jnp.bfloat16)], axis=1)


def gathered_tokens(own):
    up2 = from_offset(own, "z", 2)
    down2 = from_offset(own, "z", -2)
    far = from_offset(own, "z", 4)
    lower, upper = jnp.concatenate([own, up2]), jnp.concatenate([own, down2])
    up13 = from_offset(lower, "z", 1)
    down13 = from_offset(upper, "z", -1)
    return jnp.concatenate([own, up13, down13, up2, down2, far])


def gate_up_pieces(weights, start):
    width = weights.shape[2]
    sent = lax.dynamic_slice(weights, (start, 0, 0), (32, 2, width)).transpose(1, 0, 2)
    arrived = [from_offset(sent, "x", k) for k in (1, 3, 2)]
    three = jnp.stack(arrived, axis=1).reshape(2, 96, width)
    gate, up = three[0], three[1]
    more = [from_offset(gate, "y", -1), from_offset(up, "y", 1)]
    half = jnp.stack([three, jnp.stack(more)], axis=1).reshape(384, width)
    return half, from_offset(half, "core", 1)


def down_pieces(weights, start, rest):
    width = weights.shape[2]
    sent = jnp.stack(
        [lax.dynamic_slice(weights, (row, 2, 0), (32, 1, width)).reshape(32, width) for row in (start, rest)]
    )
    arrived = [from_offset(sent, "x", k) for k in (1, 3, 2)]
    half = jnp.stack(arrived, axis=1).reshape(192, width)
    return half, from_offset(half, "core", 1)


def dot_t(a, b):
    return lax.dot_general(a, b, (((1,), (1,)), ((), ())), preferred_element_type=jnp.float32)


def coefficients(x_index, tail):
    position = jnp.arange(512)
    third = position // 32 % 3
    offset = jnp.where(position < 128, 0, jnp.where(third == 1, 1, jnp.where(third == 2, 3, 2)))
    group = (x_index + offset) % EXPERTS
    column = jnp.arange(128)
    chosen = (column < 3 * EXPERTS) & (column % EXPERTS == group[:, None])
    return dot_t(chosen.astype(jnp.bfloat16), tail)


def gated(product, coef):
    rows = product.shape[0] // 2
    gate, up = product[:rows], product[rows:]
    return (narrow(gate / (1.0 + jnp.exp(-gate)) * up) * coef).astype(jnp.bfloat16)


def hidden_units(coef, tokens, own, half, other):
    first = jnp.einsum("hgd,nd->ghn", own, tokens, preferred_element_type=jnp.float32)
    first = first.reshape(256, -1)
    second, third = dot_t(half, tokens), dot_t(other, tokens)
    return jnp.concatenate(
        [gated(first, coef[:128]), gated(second, coef[128:320]), gated(third, coef[320:])]
    )


def returned(hidden, own, half, other):
    rows = jnp.concatenate([own, half, other])
    part = lax.dot_general(hidden, rows, (((0,), (0,)), ((), ())), preferred_element_type=jnp.float32)
    keep, up1, up3, down1, down3, up2, down2, far = part.astype(jnp.bfloat16).reshape(8, ROWS, -1)
    even = lax.axis_index("z") % 2 == 0
    wide = lambda v: v.astype(jnp.float32)
    pairs = [(i, (i + 2) % 8 if i % 2 == 0 else (i - 2) % 8) for i in range(8)]
    far = wide(lax.ppermute(far, "z", pairs))
    from_up3 = from_offset(down3, "z", 1)
    from_down3 = from_offset(up3, "z", -1)
    from_up1 = from_offset(down1, "z", 1)
    from_down1 = from_offset(up1, "z", -1)
    sum_up2 = wide(up2) + wide(from_down3) + jnp.where(even, far, 0.0)
    sum_down2 = wide(down2) + wide(from_up3) + jnp.where(even, 0.0, far)
    from_up2 = from_offset(sum_down2.astype(jnp.bfloat16), "z", 2)
    from_down2 = from_offset(sum_up2.astype(jnp.bfloat16), "z", -2)
    return (wide(keep) + wide(from_down1) + wide(from_up1)
            + wide(from_down2) + wide(from_up2)).astype(jnp.bfloat16)


def shards(tokens, expert_ids, route_weights, owner_map, expert_weights):
    width = tokens.shape[-1]
    core, parity, x_index = lax.axis_index("core"), lax.axis_index("y") % 2, lax.axis_index("x")
    start, rest = core * 64 + parity * 32, core * 64 + 32 - parity * 32
    packed = packed_tokens(tokens, expert_ids, route_weights, owner_map)
    half, other = gate_up_pieces(expert_weights, start)
    down_half, down_other = down_pieces(expert_weights, start, rest)
    gathered = gathered_tokens(packed)
    coef = coefficients(x_index, gathered[:, width:])
    own = expert_weights[:, :2]
    own_down = lax.optimization_barrier(expert_weights[:, 2])
    hidden = hidden_units(coef, gathered[:, :width], own, half, other)
    return returned(hidden, own_down, down_half, down_other).reshape(tokens.shape)


def solution(mesh):
    split = Mesh(mesh.devices.reshape(8, 2, 4, 8), AXES)
    rows = P(None, AXES, None)
    return jax.shard_map(
        shards,
        mesh=split,
        in_specs=(rows, rows, rows, P(AXES[:2]), P(AXES[2:], None, None)),
        out_specs=rows,
        check_vma=False,
    )
```
